32 devices in a mesh: lev: 2 (over x), lon: 4 (over y, core), lat: 4 (over z).
Axes of the slice: x: 2, y: 2, z: 4, core: 2. Of those that a mesh axis runs over, the one named last changes fastest.
Arguments:
- fields: bfloat16 [42, 6, 256, 512], P('lev', None, 'lat', 'lon'), may hold values from -6 to 6
- level_slot: int32 [37], replicated, may hold values from 0 to 41, as said below
- dilation: int32 [4], replicated, may hold values from 1 to 8, as said below
- lift_weight: bfloat16 [6, 128], replicated, may hold values from -2.5 to 2.5
- conv_weight: bfloat16 [4, 3, 128, 128], replicated, may hold values from -0.3125 to 0.3125
- conv_bias: float32 [4, 128], replicated, may hold values from -3 to 3
- out_weight: bfloat16 [128, 6], replicated, may hold values from -0.5 to 0.5
Outputs:
- spectra: float32 [42, 6, 2, 128, 128], P('lev', None, None, ('lon', 'lat'))
The draws below stay inside these ranges and needn't reach their ends.
Inputs may be any that keep to these rules, and one draw needn't show every extreme that they name: level_slot rises strictly; the owner of a level is its slot // 21; owners take consecutive runs of levels; each owner holds 1 to 21 levels and some owner holds exactly 21; every owner but the last fills its first slots in order, the last owner fills its last slots in order. Some layer has dilation exactly 8.
All inputs are finite; a program needn't handle non-finite values.
Results may differ from the reference program's by a relative error of at most 0.0033.
Values may be sent and summed in bfloat16 or wider, within the bound.
A program may use at most 320 MiB of HBM per device.

```python
import math
import jax
import jax.numpy as jnp
from jax import lax

F = 6
L = 37
NLON = 512
NLAT = 256
C = 128
NCONV = 4
DMAX = 8
MW = 128
NDEG = 128
LCAP = 21
SLOTS = 42
N_LEV = 2


def draw_level_slot(key, part):
    base_key = jax.random.fold_in(key, 11)
    key_full = jax.random.fold_in(base_key, 1)
    key_add = jax.random.fold_in(base_key, 2)
    full_owner = jax.random.randint(key_full, (), 0, N_LEV)
    counts = jnp.ones((N_LEV,), jnp.int32).at[full_owner].set(LCAP)
    extra = L - LCAP - (N_LEV - 1)
    owner_ids = jnp.arange(N_LEV, dtype=jnp.int32)

    def add_one(index_now, current):
        scores = jax.random.randint(jax.random.fold_in(key_add, index_now), (N_LEV,), 0, 1 << 20) * N_LEV + owner_ids
        scores = jnp.where(current < LCAP, scores, -1)
        picked = jnp.argmax(scores)
        return current.at[picked].add(1)
    counts = lax.fori_loop(0, extra, add_one, counts)
    ends = jnp.cumsum(counts)
    starts = ends - counts
    level_ids = jnp.arange(L, dtype=jnp.int32)
    owner = jnp.sum((level_ids[:, None] >= ends[None, :]).astype(jnp.int32), axis=1)
    owner_start = jnp.take(starts, owner)
    last_count = counts[N_LEV - 1]
    offset = jnp.where(owner == N_LEV - 1, LCAP - last_count, 0)
    return (owner * LCAP + level_ids - owner_start + offset).astype(jnp.int32)


def draw_dilation(key, part):
    base_key = jax.random.fold_in(key, 23)
    values = jax.random.randint(jax.random.fold_in(base_key, 1), (NCONV,), 1, DMAX + 1)
    position = jax.random.randint(jax.random.fold_in(base_key, 2), (), 0, NCONV)
    return values.at[position].set(DMAX).astype(jnp.int32)


def block_scale(own_key, dims, split, smallest, top_value):
    loudness = 1.0
    for dim, parts in split:
        steps = jax.random.uniform(jax.random.fold_in(jax.random.fold_in(own_key, 6), dim), (parts,), jnp.float32, smallest / len(split), top_value / len(split))
        loudness = loudness * jnp.repeat(jnp.exp(steps), dims[dim] // parts).reshape((-1,) + (1,) * (len(dims) - 1 - dim))
    return loudness


def noise(stream_key, shape, deviation, limit, pieces=(), held_as=jnp.bfloat16):
    entries = jax.random.normal(stream_key, shape, jnp.float32) * deviation
    if len(pieces) > 0:
        entries = block_scale(stream_key, shape, pieces, -0.22, 0.18) * entries
    return jnp.clip(entries, min=-limit, max=limit).astype(held_as)


def setup_inputs(seed: int = 0) -> dict:
    streams_of = jax.random.split(jax.random.key(seed), 8)
    return {
        "fields": noise(streams_of[0], (SLOTS, F, NLAT, NLON), 1.0, 6.0, ((0, 2), (2, 4), (3, 4))),
        "level_slot": draw_level_slot(jax.random.fold_in(streams_of[7], 71), 0),
        "dilation": draw_dilation(jax.random.fold_in(streams_of[7], 71), 0),
        "lift_weight": noise(streams_of[3], (F, C), F ** -0.5, 2.5),
        "conv_weight": noise(streams_of[4], (NCONV, 3, C, C), (3 * C) ** -0.5, 0.3125),
        "conv_bias": noise(streams_of[5], (NCONV, C), 0.5, 3.0, (), jnp.float32),
        "out_weight": noise(streams_of[6], (C, F), C ** -0.5, 0.5),
    }


def legendre_table(orders, lat_angle, degrees):
    sin_lat = jnp.sin(lat_angle)
    cos_lat = jnp.cos(lat_angle)
    counter = jnp.arange(1, degrees).astype(jnp.float32)
    log_steps = 0.5 * jnp.log((2.0 * counter + 1.0) / (2.0 * counter))
    log_table = jnp.concatenate([jnp.zeros((1,), jnp.float32), jnp.cumsum(log_steps)])
    one_hot = (orders[:, None] == jnp.arange(degrees, dtype=jnp.int32)[None, :]).astype(jnp.float32)
    log_start = lax.optimization_barrier(jnp.sum(one_hot * log_table[None, :], axis=1))
    order_f = orders.astype(jnp.float32)[:, None]
    diagonal = jnp.sqrt(jnp.float32(0.5)) * jnp.exp(log_start[:, None] + order_f * jnp.log(cos_lat)[None, :])
    orders_col = orders[:, None]

    def advance(carry, degree):
        prev_one, prev_two = carry
        deg_f = degree.astype(jnp.float32)
        ratio_up = jnp.sqrt((4.0 * deg_f * deg_f - 1.0) / jnp.maximum(deg_f * deg_f - order_f * order_f, 1.0))
        back_num = jnp.maximum((deg_f - 1.0) * (deg_f - 1.0) - order_f * order_f, 0.0)
        ratio_back = jnp.sqrt(back_num / jnp.maximum(4.0 * (deg_f - 1.0) * (deg_f - 1.0) - 1.0, 1.0))
        recur = ratio_up * (sin_lat[None, :] * prev_one - ratio_back * prev_two)
        first = jnp.sqrt(2.0 * order_f + 3.0) * sin_lat[None, :] * prev_one
        fresh = jnp.where(degree == orders_col, diagonal, jnp.where(degree == orders_col + 1, first, jnp.where(degree > orders_col + 1, recur, jnp.zeros_like(recur))))
        return ((fresh, prev_one), fresh)
    empty_rows = jnp.zeros_like(diagonal)
    final_pair, stacked = lax.scan(advance, (empty_rows, empty_rows), jnp.arange(degrees, dtype=jnp.int32))
    return jnp.transpose(stacked, (1, 0, 2))

def latitudes(lat_ids, lat_count):
    return -0.5 * math.pi + (lat_ids.astype(jnp.float32) + 0.5) * (math.pi / lat_count)

def quad_weights(lat_angle, lat_count):
    return jnp.cos(lat_angle) * math.sqrt(2.0 * math.pi / lat_count)

def column_net(col_block, dilation, lift_weight, conv_weight, conv_bias, out_weight):
    levels = col_block.shape[0]
    hidden = jnp.einsum('lfq,fc->lqc', col_block.astype(jnp.float32), lift_weight.astype(jnp.float32)).astype(jnp.bfloat16)
    for layer in range(NCONV):
        spacing = dilation[layer]
        padded = jnp.pad(hidden, ((DMAX, DMAX), (0, 0), (0, 0)))
        lower_lev = lax.dynamic_slice_in_dim(padded, (DMAX - spacing).astype(jnp.int32), levels, 0)
        upper_lev = lax.dynamic_slice_in_dim(padded, (DMAX + spacing).astype(jnp.int32), levels, 0)
        taps = conv_weight[layer].astype(jnp.float32)
        branch_sum = jnp.einsum('lqc,cd->lqd', lower_lev.astype(jnp.float32), taps[0]) + jnp.einsum('lqc,cd->lqd', hidden.astype(jnp.float32), taps[1]) + jnp.einsum('lqc,cd->lqd', upper_lev.astype(jnp.float32), taps[2]) + conv_bias[layer][None, None, :]
        hidden = (hidden.astype(jnp.float32) + jax.nn.gelu(branch_sum, approximate=True)).astype(jnp.bfloat16)
    correction = jnp.einsum('lqc,cf->lfq', hidden.astype(jnp.float32), out_weight.astype(jnp.float32))
    return (col_block.astype(jnp.float32) + correction).astype(jnp.bfloat16)

def reference(fields, level_slot, dilation, lift_weight, conv_weight, conv_bias, out_weight):
    columns = jnp.take(fields, level_slot, axis=0)
    rows_major = jnp.transpose(columns, (2, 0, 1, 3))

    def per_row(col_block):
        return column_net(col_block, dilation, lift_weight, conv_weight, conv_bias, out_weight)
    corrected = jnp.transpose(lax.map(per_row, rows_major), (1, 2, 0, 3))
    level_grid = jnp.zeros(fields.shape, jnp.bfloat16).at[level_slot].set(corrected)
    wave_ids = jnp.arange(MW, dtype=jnp.int32)
    lon_ids = jnp.arange(NLON, dtype=jnp.int32)
    phase_arg = (wave_ids[:, None] * lon_ids[None, :] % NLON).astype(jnp.float32) * (2.0 * math.pi / NLON)
    norm_scale = 1.0 / math.sqrt(NLON)
    cosine = jnp.cos(phase_arg) * norm_scale
    sine_tab = -jnp.sin(phase_arg) * norm_scale
    grid_wide = level_grid.astype(jnp.float32)
    real_part = jnp.einsum('sfyx,mx->msfy', grid_wide, cosine, precision=lax.Precision.HIGHEST)
    imag_part = jnp.einsum('sfyx,mx->msfy', grid_wide, sine_tab, precision=lax.Precision.HIGHEST)
    fourier = jnp.stack([real_part, imag_part], axis=1)
    lat_angle = latitudes(jnp.arange(NLAT, dtype=jnp.int32), NLAT)
    leg_table = legendre_table(wave_ids, lat_angle, NDEG) * quad_weights(lat_angle, NLAT)[None, None, :]
    return jnp.einsum('mnk,mrsfk->sfrmn', leg_table, fourier, precision=lax.Precision.HIGHEST)
```

```python
import math

import jax
import jax.numpy as jnp
import numpy as np
from jax import lax
from jax.experimental import pallas as pl
from jax.experimental.pallas import tpu as pltpu
from jax.sharding import PartitionSpec as P

NLON = 512
NLAT = 256
DMAX = 8
MW = 128
NDEG = 128


def legendre_table(orders, lat_angle, degrees):
    sin_lat = jnp.sin(lat_angle)
    cos_lat = jnp.cos(lat_angle)
    counter = jnp.arange(1, degrees).astype(jnp.float32)
    log_steps = 0.5 * jnp.log((2.0 * counter + 1.0) / (2.0 * counter))
    log_table = jnp.concatenate([jnp.zeros((1,), jnp.float32), jnp.cumsum(log_steps)])
    one_hot = (orders[:, None] == jnp.arange(degrees, dtype=jnp.int32)[None, :]).astype(jnp.float32)
    log_start = jnp.sum(one_hot * log_table[None, :], axis=1)
    order_f = orders.astype(jnp.float32)[:, None]
    diagonal = jnp.sqrt(jnp.float32(0.5)) * jnp.exp(
        log_start[:, None] + order_f * jnp.log(cos_lat)[None, :]
    )
    count, lats = diagonal.shape
    order_full = jnp.broadcast_to(order_f, (count, lats))
    sin_full = jnp.broadcast_to(sin_lat[None, :], (count, lats))
    return pl.pallas_call(
        legendre_kernel,
        out_shape=jax.ShapeDtypeStruct((degrees, count, lats), jnp.float32),
        name="legendre",
    )(order_full, sin_full, diagonal)


def legendre_kernel(order_ref, sin_ref, diag_ref, out_ref):
    order = order_ref[...]
    sin_lat = sin_ref[...]
    diagonal = diag_ref[...]
    first_scale = jnp.sqrt(2.0 * order + 3.0) * sin_lat
    zero = order * 0.0

    def advance(degree, carry):
        prev_one, prev_two = carry
        deg = zero + degree.astype(jnp.float32)
        ratio_up = jnp.sqrt((4.0 * deg * deg - 1.0) / jnp.maximum(deg * deg - order * order, 1.0))
        before = deg - 1.0
        back_num = jnp.maximum(before * before - order * order, 0.0)
        ratio_back = jnp.sqrt(back_num / jnp.maximum(4.0 * before * before - 1.0, 1.0))
        recur = ratio_up * (sin_lat * prev_one - ratio_back * prev_two)
        first = first_scale * prev_one
        fresh = jnp.where(
            deg == order,
            diagonal,
            jnp.where(deg == order + 1.0, first, jnp.where(deg > order + 1.0, recur, zero)),
        )
        out_ref[degree] = fresh
        return fresh, prev_one

    lax.fori_loop(0, out_ref.shape[0], advance, (zero, zero))


def latitudes(lat_ids, lat_count):
    return -0.5 * math.pi + (lat_ids.astype(jnp.float32) + 0.5) * (math.pi / lat_count)


def quad_weights(lat_angle, lat_count):
    return jnp.cos(lat_angle) * math.sqrt(2.0 * math.pi / lat_count)


def column_kernel(dil_ref, col_ref, lift_ref, conv_ref, bias_ref, out_w_ref, out_ref, ping, pong):
    levels, _, tile = col_ref.shape
    channels = lift_ref.shape[1]
    layers = conv_ref.shape[0]

    @pl.when(pl.program_id(0) == 0)
    def _():
        edge = jnp.zeros((DMAX, tile, channels), jnp.bfloat16)
        for buf in (ping, pong):
            buf[pl.ds(0, DMAX)] = edge
            buf[pl.ds(DMAX + levels, DMAX)] = edge

    lift = lift_ref[...]

    def lift_level(lev, carry):
        hidden = lax.dot_general(
            col_ref[lev], lift, (((0,), (0,)), ((), ())), preferred_element_type=jnp.float32
        )
        ping[DMAX + lev] = hidden.astype(jnp.bfloat16)
        return carry

    lax.fori_loop(0, levels, lift_level, 0)

    inner = math.sqrt(2.0 / math.pi)
    for layer in range(layers):
        src, dst = (ping, pong) if layer % 2 == 0 else (pong, ping)
        spacing = dil_ref[layer]

        def conv_level(lev, carry, src=src, dst=dst, spacing=spacing, layer=layer):
            own = src[DMAX + lev]
            taps = jnp.concatenate(
                [src[DMAX + lev - spacing], own, src[DMAX + lev + spacing]], axis=1
            )
            value = (
                jnp.dot(taps, conv_ref[layer], preferred_element_type=jnp.float32)
                + bias_ref[pl.ds(layer, 1), :]
            )
            curve = jnp.tanh(value * (inner + (inner * 0.044715) * (value * value)))
            half = 0.5 * value
            fresh = (own.astype(jnp.float32) + (half + half * curve)).astype(jnp.bfloat16)
            if layer + 1 < layers:
                dst[DMAX + lev] = fresh
            else:
                correction = lax.dot_general(
                    out_w_ref[...], fresh, (((1,), (1,)), ((), ())),
                    preferred_element_type=jnp.float32,
                )
                out_ref[lev] = (col_ref[lev].astype(jnp.float32) + correction).astype(jnp.bfloat16)
            return carry

        lax.fori_loop(0, levels, conv_level, 0)


def column_net(col_flat, dilation, lift_weight, conv_weight, conv_bias, out_weight):
    levels, field_count, columns = col_flat.shape
    layers, taps, channels, _ = conv_weight.shape
    tile = min(512, columns)
    while columns % tile:
        tile //= 2
    whole = lambda *dims: pl.BlockSpec(dims, lambda i, d: (0,) * len(dims))
    moving = pl.BlockSpec((levels, field_count, tile), lambda i, d: (0, 0, i))
    scratch = pltpu.VMEM((levels + 2 * DMAX, tile, channels), jnp.bfloat16)
    return pl.pallas_call(
        column_kernel,
        out_shape=jax.ShapeDtypeStruct(col_flat.shape, jnp.bfloat16),
        grid_spec=pltpu.PrefetchScalarGridSpec(
            num_scalar_prefetch=1,
            grid=(columns // tile,),
            in_specs=[
                moving,
                whole(field_count, channels),
                whole(layers, taps * channels, channels),
                whole(layers, channels),
                whole(field_count, channels),
            ],
            out_specs=moving,
            scratch_shapes=[scratch, scratch],
        ),
        compiler_params=pltpu.CompilerParams(vmem_limit_bytes=48 * 1024 * 1024),
        name="column_net",
    )(
        dilation,
        col_flat,
        lift_weight,
        conv_weight.reshape(layers, taps * channels, channels),
        conv_bias,
        jnp.transpose(out_weight),
    )


def on_device(fields, level_slot, dilation, lift_weight, conv_weight, conv_bias, out_weight):
    slot_cap, field_count, lat_loc, lon_loc = fields.shape
    received = lax.all_to_all(fields, "lev", split_axis=3, concat_axis=0, tiled=True)
    lon_part = received.shape[3]
    columns = jnp.take(received, level_slot, axis=0)
    levels = columns.shape[0]
    col_flat = columns.reshape(levels, field_count, lat_loc * lon_part)
    corrected = column_net(col_flat, dilation, lift_weight, conv_weight, conv_bias, out_weight)
    corrected = corrected.reshape(levels, field_count, lat_loc, lon_part)
    slotted = jnp.zeros(received.shape, jnp.bfloat16).at[level_slot].set(corrected)
    level_grid = lax.all_to_all(slotted, "lev", split_axis=0, concat_axis=3, tiled=True)
    norm_scale = 1.0 / math.sqrt(NLON)
    lat_groups = lax.axis_size("lat")
    lon_groups = lax.axis_size("lon")
    owners = lat_groups * lon_groups
    owner_index = lax.axis_index("lon") * lat_groups + lax.axis_index("lat")
    rows = jnp.transpose(
        level_grid.reshape(slot_cap * field_count, lat_loc, lon_loc), (1, 0, 2)
    )
    circle = lax.all_to_all(rows, "lon", split_axis=0, concat_axis=2, tiled=True)
    sub_rows = circle.shape[0]
    waves = np.arange(MW, dtype=np.int64)[:, None] * np.arange(NLON, dtype=np.int64)[None, :] % NLON
    phase = waves.astype(np.float64) * (2.0 * math.pi / NLON)
    table = np.stack([np.cos(phase), -np.sin(phase)], axis=1).reshape(2 * MW, NLON) * norm_scale
    table_high = table.astype(jnp.bfloat16)
    table_low = (table - table_high.astype(np.float64)).astype(jnp.bfloat16)
    wide = lambda part: jnp.einsum(
        "wx,lcx->wlc", jnp.asarray(part), circle, preferred_element_type=jnp.float32
    )
    fourier = (wide(table_high) + wide(table_low)).astype(jnp.bfloat16)
    own_count = MW // owners
    fourier = fourier.reshape(owners, own_count, 2, sub_rows, slot_cap * field_count)
    coef = lax.all_to_all(fourier, ("lon", "lat"), split_axis=0, concat_axis=0, tiled=True)
    position = jnp.arange(NLAT, dtype=jnp.int32)
    source_id = position // sub_rows
    within = position % sub_rows
    source_lon = source_id // lat_groups
    source_lat = source_id % lat_groups
    order_ids = source_lat * lat_loc + source_lon * sub_rows + within
    order_angle = latitudes(order_ids, NLAT)
    order_weight = quad_weights(order_angle, NLAT)
    wave_ids = owner_index * own_count + jnp.arange(own_count, dtype=jnp.int32)
    leg_table = legendre_table(wave_ids, order_angle, NDEG) * order_weight[None, None, :]
    leg_rows = jnp.transpose(leg_table, (1, 0, 2))
    leg_high = leg_rows.astype(jnp.bfloat16)
    leg_low = (leg_rows - leg_high.astype(jnp.float32)).astype(jnp.bfloat16)
    coef = jnp.transpose(coef, (1, 2, 4, 0, 3)).reshape(
        own_count, 2 * slot_cap * field_count, NLAT
    )
    both = jnp.concatenate([leg_high, leg_low], axis=1)
    sums = jnp.einsum("mck,mnk->mcn", coef, both, preferred_element_type=jnp.float32)
    spectra = (sums[..., :NDEG] + sums[..., NDEG:]).reshape(
        own_count, 2, slot_cap, field_count, NDEG
    )
    return jnp.transpose(spectra, (2, 3, 1, 0, 4))


def solution(mesh):
    placed = (P("lev", None, "lat", "lon"), P(), P(), P(), P(), P(), P())
    return jax.shard_map(
        on_device,
        mesh=mesh,
        in_specs=placed,
        out_specs=P("lev", None, None, ("lon", "lat"), None),
        check_vma=False,
    )
```

```python
import math

import jax
import jax.numpy as jnp
import numpy as np
from jax import lax
from jax.experimental import pallas as pl
from jax.experimental.pallas import tpu as pltpu
from jax.sharding import PartitionSpec as P

NLON = 512
NLAT = 256
DMAX = 8
MW = 128
NDEG = 128


def legendre_table(orders, lat_angle, degrees):
    sin_lat = jnp.sin(lat_angle)
    cos_lat = jnp.cos(lat_angle)
    counter = jnp.arange(1, degrees).astype(jnp.float32)
    log_steps = 0.5 * jnp.log((2.0 * counter + 1.0) / (2.0 * counter))
    log_table = jnp.concatenate([jnp.zeros((1,), jnp.float32), jnp.cumsum(log_steps)])
    one_hot = (orders[:, None] == jnp.arange(degrees, dtype=jnp.int32)[None, :]).astype(jnp.float32)
    log_start = jnp.sum(one_hot * log_table[None, :], axis=1)
    order_f = orders.astype(jnp.float32)[:, None]
    diagonal = jnp.sqrt(jnp.float32(0.5)) * jnp.exp(
        log_start[:, None] + order_f * jnp.log(cos_lat)[None, :]
    )
    count, lats = diagonal.shape
    order_full = jnp.broadcast_to(order_f, (count, lats))
    sin_full = jnp.broadcast_to(sin_lat[None, :], (count, lats))
    return pl.pallas_call(
        legendre_kernel,
        out_shape=jax.ShapeDtypeStruct((degrees, count, lats), jnp.float32),
        name="legendre",
    )(order_full, sin_full, diagonal)


def legendre_kernel(order_ref, sin_ref, diag_ref, out_ref):
    order = order_ref[...]
    sin_lat = sin_ref[...]
    diagonal = diag_ref[...]
    first_scale = jnp.sqrt(2.0 * order + 3.0) * sin_lat
    zero = order * 0.0

    def advance(degree, carry):
        prev_one, prev_two = carry
        deg = zero + degree.astype(jnp.float32)
        ratio_up = jnp.sqrt((4.0 * deg * deg - 1.0) / jnp.maximum(deg * deg - order * order, 1.0))
        before = deg - 1.0
        back_num = jnp.maximum(before * before - order * order, 0.0)
        ratio_back = jnp.sqrt(back_num / jnp.maximum(4.0 * before * before - 1.0, 1.0))
        recur = ratio_up * (sin_lat * prev_one - ratio_back * prev_two)
        first = first_scale * prev_one
        fresh = jnp.where(
            deg == order,
            diagonal,
            jnp.where(deg == order + 1.0, first, jnp.where(deg > order + 1.0, recur, zero)),
        )
        out_ref[degree] = fresh
        return fresh, prev_one

    lax.fori_loop(0, out_ref.shape[0], advance, (zero, zero))


def latitudes(lat_ids, lat_count):
    return -0.5 * math.pi + (lat_ids.astype(jnp.float32) + 0.5) * (math.pi / lat_count)


def quad_weights(lat_angle, lat_count):
    return jnp.cos(lat_angle) * math.sqrt(2.0 * math.pi / lat_count)


def column_kernel(dil_ref, pair_ref, count_ref, col_ref, lift_ref, conv_ref, bias_ref, out_w_ref, out_ref, ping, pong):
    levels, _, tile = col_ref.shape
    channels = lift_ref.shape[1]
    layers = conv_ref.shape[0]
    spare = levels + 3 * DMAX

    @pl.when(pl.program_id(0) == 0)
    def _():
        edge = jnp.zeros((DMAX, tile, channels), jnp.bfloat16)
        for buf in (ping, pong):
            buf[pl.ds(0, DMAX)] = edge
            buf[pl.ds(DMAX + levels, DMAX)] = edge
            buf[pl.ds(2 * DMAX + levels, DMAX)] = edge

    lift = lift_ref[...]

    def lift_level(lev, carry):
        hidden = lax.dot_general(
            col_ref[lev], lift, (((0,), (0,)), ((), ())), preferred_element_type=jnp.float32
        )
        ping[DMAX + lev] = hidden.astype(jnp.bfloat16)
        return carry

    lax.fori_loop(0, levels, lift_level, 0)

    inner = math.sqrt(2.0 / math.pi)
    for layer in range(layers):
        src, dst = (ping, pong) if layer % 2 == 0 else (pong, ping)
        spacing = dil_ref[layer]

        def conv_pair(pair, carry, src=src, dst=dst, spacing=spacing, layer=layer):
            low = pair_ref[layer, pair]
            high = low + spacing
            own_low = src[DMAX + low]
            own_high = src[DMAX + high]
            taps = jnp.concatenate(
                [src[DMAX + low - spacing], own_low, own_high, src[DMAX + high + spacing]], axis=1
            )
            value = (
                jnp.dot(taps, conv_ref[layer], preferred_element_type=jnp.float32)
                + bias_ref[pl.ds(layer, 1), :]
            )
            curve = jnp.tanh(value * (inner + (inner * 0.044715) * (value * value)))
            half = 0.5 * value
            gelu = half + half * curve
            fresh_low = (own_low.astype(jnp.float32) + gelu[:, :channels]).astype(jnp.bfloat16)
            fresh_high = (own_high.astype(jnp.float32) + gelu[:, channels:]).astype(jnp.bfloat16)
            dst[DMAX + low] = fresh_low
            dst[jnp.where(high < levels, DMAX + high, spare)] = fresh_high
            return carry

        lax.fori_loop(0, count_ref[layer], conv_pair, 0)

    last = ping if layers % 2 == 0 else pong

    def project_level(lev, carry):
        correction = lax.dot_general(
            out_w_ref[...], last[DMAX + lev], (((1,), (1,)), ((), ())),
            preferred_element_type=jnp.float32,
        )
        out_ref[lev] = (col_ref[lev].astype(jnp.float32) + correction).astype(jnp.bfloat16)
        return carry

    lax.fori_loop(0, levels, project_level, 0)


def column_net(col_flat, dilation, lift_weight, conv_weight, conv_bias, out_weight):
    levels, field_count, columns = col_flat.shape
    layers, taps, channels, _ = conv_weight.shape
    tile = min(512, columns)
    while columns % tile:
        tile //= 2
    flat = conv_weight.reshape(layers, taps * channels, channels)
    blank = jnp.zeros((layers, channels, channels), conv_weight.dtype)
    paired = jnp.concatenate(
        [jnp.concatenate([flat, blank], axis=1), jnp.concatenate([blank, flat], axis=1)], axis=2
    )
    level_ids = jnp.arange(levels, dtype=jnp.int32)[None, :]
    is_low = (level_ids // dilation[:, None]) % 2 == 0
    counts = jnp.sum(is_low.astype(jnp.int32), axis=1)
    pairs = jnp.sort(jnp.where(is_low, level_ids, levels), axis=1)
    whole = lambda *dims: pl.BlockSpec(dims, lambda i, *d: (0,) * len(dims))
    moving = pl.BlockSpec((levels, field_count, tile), lambda i, *d: (0, 0, i))
    scratch = pltpu.VMEM((levels + 3 * DMAX + 1, tile, channels), jnp.bfloat16)
    return pl.pallas_call(
        column_kernel,
        out_shape=jax.ShapeDtypeStruct(col_flat.shape, jnp.bfloat16),
        grid_spec=pltpu.PrefetchScalarGridSpec(
            num_scalar_prefetch=3,
            grid=(columns // tile,),
            in_specs=[
                moving,
                whole(field_count, channels),
                whole(layers, (taps + 1) * channels, 2 * channels),
                whole(layers, 2 * channels),
                whole(field_count, channels),
            ],
            out_specs=moving,
            scratch_shapes=[scratch, scratch],
        ),
        compiler_params=pltpu.CompilerParams(vmem_limit_bytes=48 * 1024 * 1024),
        name="column_net",
    )(
        dilation,
        pairs,
        counts,
        col_flat,
        lift_weight,
        paired,
        jnp.concatenate([conv_bias, conv_bias], axis=1),
        jnp.transpose(out_weight),
    )


def on_device(fields, level_slot, dilation, lift_weight, conv_weight, conv_bias, out_weight):
    slot_cap, field_count, lat_loc, lon_loc = fields.shape
    received = lax.all_to_all(fields, "lev", split_axis=3, concat_axis=0, tiled=True)
    lon_part = received.shape[3]
    columns = jnp.take(received, level_slot, axis=0)
    levels = columns.shape[0]
    col_flat = columns.reshape(levels, field_count, lat_loc * lon_part)
    corrected = column_net(col_flat, dilation, lift_weight, conv_weight, conv_bias, out_weight)
    corrected = corrected.reshape(levels, field_count, lat_loc, lon_part)
    slotted = jnp.zeros(received.shape, jnp.bfloat16).at[level_slot].set(corrected)
    level_grid = lax.all_to_all(slotted, "lev", split_axis=0, concat_axis=3, tiled=True)
    norm_scale = 1.0 / math.sqrt(NLON)
    lat_groups = lax.axis_size("lat")
    lon_groups = lax.axis_size("lon")
    owners = lat_groups * lon_groups
    owner_index = lax.axis_index("lon") * lat_groups + lax.axis_index("lat")
    rows = jnp.transpose(
        level_grid.reshape(slot_cap * field_count, lat_loc, lon_loc), (1, 0, 2)
    )
    circle = lax.all_to_all(rows, "lon", split_axis=0, concat_axis=2, tiled=True)
    sub_rows = circle.shape[0]
    waves = np.arange(MW, dtype=np.int64)[:, None] * np.arange(NLON, dtype=np.int64)[None, :] % NLON
    phase = waves.astype(np.float64) * (2.0 * math.pi / NLON)
    table = np.stack([np.cos(phase), -np.sin(phase)], axis=1).reshape(2 * MW, NLON) * norm_scale
    table_high = table.astype(jnp.bfloat16)
    table_low = (table - table_high.astype(np.float64)).astype(jnp.bfloat16)
    wide = lambda part: jnp.einsum(
        "wx,lcx->wlc", jnp.asarray(part), circle, preferred_element_type=jnp.float32
    )
    fourier = (wide(table_high) + wide(table_low)).astype(jnp.bfloat16)
    own_count = MW // owners
    fourier = fourier.reshape(owners, own_count, 2, sub_rows, slot_cap * field_count)
    coef = lax.all_to_all(fourier, ("lon", "lat"), split_axis=0, concat_axis=0, tiled=True)
    position = jnp.arange(NLAT, dtype=jnp.int32)
    source_id = position // sub_rows
    within = position % sub_rows
    source_lon = source_id // lat_groups
    source_lat = source_id % lat_groups
    order_ids = source_lat * lat_loc + source_lon * sub_rows + within
    order_angle = latitudes(order_ids, NLAT)
    order_weight = quad_weights(order_angle, NLAT)
    wave_ids = owner_index * own_count + jnp.arange(own_count, dtype=jnp.int32)
    leg_table = legendre_table(wave_ids, order_angle, NDEG) * order_weight[None, None, :]
    leg_rows = jnp.transpose(leg_table, (1, 0, 2))
    leg_high = leg_rows.astype(jnp.bfloat16)
    leg_low = (leg_rows - leg_high.astype(jnp.float32)).astype(jnp.bfloat16)
    coef = jnp.transpose(coef, (1, 2, 4, 0, 3)).reshape(
        own_count, 2 * slot_cap * field_count, NLAT
    )
    both = jnp.concatenate([leg_high, leg_low], axis=1)
    sums = jnp.einsum("mck,mnk->mcn", coef, both, preferred_element_type=jnp.float32)
    spectra = (sums[..., :NDEG] + sums[..., NDEG:]).reshape(
        own_count, 2, slot_cap, field_count, NDEG
    )
    return jnp.transpose(spectra, (2, 3, 1, 0, 4))


def solution(mesh):
    placed = (P("lev", None, "lat", "lon"), P(), P(), P(), P(), P(), P())
    return jax.shard_map(
        on_device,
        mesh=mesh,
        in_specs=placed,
        out_specs=P("lev", None, None, ("lon", "lat"), None),
        check_vma=False,
    )
```
